128 devices in a mesh: dp: 4 (over y), pipe: 4 (over z_lo, core), ctx: 8 (over z_hi, x).
Axes of the slice: x: 4, y: 4, z: 4 (z_hi: 2, z_lo: 2; z = z_hi * 2 + z_lo), core: 2. Of those that a mesh axis runs over, the one named last changes fastest.
Arguments:
- acts: bfloat16 [4, 4, 4, 2176, 8192], P('dp', 'pipe', None, 'ctx'), may hold values from -0.125 to 0.125
- key_grads: bfloat16 [4, 4, 4, 2176, 512], P('dp', 'pipe', None, 'ctx'), may hold values from -6 to 6
- weights: bfloat16 [4, 8192, 512], P('pipe', 'ctx'), may hold values from -0.25 to 0.25
- b_slot: int32 [4], P('pipe'), may hold values from 0 to 3
- cycle: int32 [32], replicated, may hold values from 0 to 31, each once
Outputs:
- passed_grad: bfloat16 [4, 4, 2176, 8192], P('dp', 'pipe', 'ctx')
- weight_grad: float32 [4, 8192, 512], P('pipe', 'ctx')
The draws below stay inside these ranges and needn't reach their ends.
Inputs may be any that keep to these rules, and one draw needn't show every extreme that they name: `cycle`: each value once.
All inputs are finite; a program needn't handle non-finite values.
Results may differ from the reference program's by a relative error of at most 0.001.
Values may be sent and summed in bfloat16 or wider, within the bound.
A program may use at most 192 MiB of HBM per device.

```python
import jax
import jax.numpy as jnp
from jax import lax

D = 8192
KW = 512
MB = 4
ROWS = 272
SEQ_ROWS = 2176
PIECES = 32
N_DP = 4
N_PIPE = 4
N_CTX = 8


def set_ends(entries, key, low, high):
    shape = entries.shape
    place = [jax.random.randint(jax.random.fold_in(key, axis), (), 0, shape[axis]) for axis in range(len(shape))]
    entries = entries.at[tuple(place)].set(low)
    longest = shape.index(max(shape))
    place[longest] = (place[longest] + 1) % shape[longest]
    return entries.at[tuple(place)].set(high)


def spiked(drawn, rng, source, target, blocks, factor):
    def block_of(dim):
        return (jnp.arange(drawn.shape[dim]) // (drawn.shape[dim] // blocks)).reshape((-1,) + (1,) * (drawn.ndim - 1 - dim))

    one_side = jax.random.permutation(rng, blocks)[block_of(target)]
    other_side = (block_of(target) + blocks // 2) % blocks
    return jnp.where((block_of(source) == one_side) | (block_of(source) == other_side), factor * drawn, drawn)


def levels(stream_key, extent, split, low, largest):
    def one(dim, parts):
        steps = jax.random.uniform(jax.random.fold_in(jax.random.fold_in(stream_key, 6), dim), (parts,), jnp.float32, low / len(split), largest / len(split))
        return jnp.repeat(jnp.exp(steps), extent[dim] // parts).reshape((-1,) + (1,) * (len(extent) - dim - 1))

    factor_of = one(*split[0])
    for cut in split[1:]:
        factor_of = factor_of * one(*cut)
    return factor_of


def noise(key, dims, spread, bound, split=(), kind=jnp.bfloat16):
    array = spread * jax.random.normal(key, dims, jnp.float32)
    if split:
        array = array * levels(key, dims, split, -0.22, 0.18)
    return jnp.clip(array, -bound, bound).astype(kind)


def gaussian_with(key, dims, scale, limit, split, heavy, kind=jnp.bfloat16):
    array = scale * jax.random.normal(key, dims, jnp.float32)
    if split:
        array = array * levels(key, dims, split, -0.22, 0.18)
    return jnp.clip(spiked(array, jax.random.fold_in(key, 3), *heavy), -limit, limit).astype(kind)


def setup_inputs(seed: int = 0) -> dict:
    keys = jax.random.split(jax.random.key(seed), 6)
    acts = gaussian_with(keys[0], (N_DP, N_PIPE, MB, SEQ_ROWS, D), (1.0 / (N_DP * (MB - 1) * ROWS * N_CTX) ** 0.5), 0.125, ((0, 4), (1, 4), (3, 8)), (3, 4, 8, 2.0))
    key_grads = noise(keys[1], (N_DP, N_PIPE, MB, SEQ_ROWS, KW), 1.0, 6.0, ((0, 4), (1, 4), (3, 8)))
    weights = noise(keys[2], (N_PIPE, D, KW), KW ** -0.5, 0.25, ((0, 4), (1, 8)))
    b_slot = set_ends(jax.random.randint(keys[3], (N_PIPE,), 0, MB), jax.random.fold_in(keys[3], 1), 0, MB - 1).astype(jnp.int32)
    cycle = jax.random.permutation(keys[4], PIECES).astype(jnp.int32)
    return dict(acts=acts, key_grads=key_grads, weights=weights, b_slot=b_slot, cycle=cycle)


def reference(acts, key_grads, weights, b_slot, cycle):
    section_list = []
    grad_list = []
    micro = jnp.arange(MB, dtype=jnp.int32)
    for section in range(N_PIPE):
        slot_index = b_slot[section]
        current = lax.dynamic_index_in_dim(key_grads[:, section], slot_index, 1, keepdims=False).reshape(-1, KW)
        section_grad = lax.dot_general(current, weights[section], (((1,), (1,)), ((), ())), preferred_element_type=jnp.float32).astype(jnp.bfloat16)
        section_list.append(section_grad.reshape(N_DP, SEQ_ROWS, D))
        keeper = (micro != slot_index)[None, :, None, None]
        masked = jnp.where(keeper, key_grads[:, section], jnp.zeros((), key_grads.dtype)).reshape(-1, KW)
        full_grad = lax.dot_general(acts[:, section].reshape(-1, D), masked, (((0,), (0,)), ((), ())), preferred_element_type=jnp.float32)
        grad_list.append(full_grad.reshape(PIECES, D // PIECES, KW)[cycle].reshape(D, KW))
    shifted = section_list[1:] + [jnp.zeros_like(section_list[0])]
    return jnp.stack(shifted, axis=1), jnp.stack(grad_list, axis=0)
```

```python
import functools

import jax
import jax.numpy as jnp
from jax import lax
from jax.experimental import pallas as pl
from jax.experimental.pallas import tpu as pltpu
from jax.sharding import PartitionSpec as P

MESH = pl.DeviceIdType.MESH
TOP = 32700.0
LEAD = 16


def wrap(value):
    return lax.rem(value + 8, 4)


def kernel(
    picks_ref,
    cycle_ref,
    acts_hbm,
    grads_hbm,
    weights_hbm,
    passed_hbm,
    pieces_hbm,
    acts,
    grads,
    weights,
    chosen,
    tokens,
    results,
    part,
    first_in,
    first_pair,
    second_in,
    second_pair,
    z_in,
    z_out,
    last,
    wide,
    load_sem,
    piece_sem,
    token_send,
    token_recv,
    weight_send,
    weight_recv,
    result_send,
    result_recv,
    one_send,
    one_recv,
    pair_send,
    pair_recv,
    z_send,
    z_recv,
    last_send,
    last_recv,
    keep_sem,
):
    y = lax.axis_index("dp")
    p = lax.axis_index("pipe")
    c = lax.axis_index("ctx")
    zh = lax.div(c, 4)
    x = lax.rem(c, 4)
    piece_rows = wide.shape[0]
    rows = grads.shape[1]
    block = weights.shape[1]
    groups = piece_rows // LEAD

    def at(dy=0, dx=0, dz=0, dp=0):
        zz = lax.rem(zh + dz, 2)
        return (wrap(y + dy), p + dp, zz * 4 + wrap(x + dx))

    load_g = pltpu.make_async_copy(grads_hbm, grads, load_sem.at[0])
    load_w = pltpu.make_async_copy(weights_hbm, weights.at[0], load_sem.at[1])

    def load_piece(n):
        start = pl.multiple_of(n * piece_rows, piece_rows)
        return pltpu.make_async_copy(
            acts_hbm.at[:, :, pl.ds(start, piece_rows)], acts.at[n], piece_sem.at[n]
        )

    load_g.start()
    load_w.start()

    @pl.loop(0, acts.shape[0])
    def _(n):
        load_piece(n).start()


    barrier = pltpu.get_barrier_semaphore()
    peers = [at(dy=1), at(dy=2), at(dy=3), at(dx=1), at(dx=2), at(dx=3), at(dz=1)]
    for peer in peers:
        pl.semaphore_signal(barrier, 1, device_id=peer, device_id_type=MESH)

    @pl.when(p > 0)
    def _():
        for off in range(4):
            pl.semaphore_signal(barrier, 1, device_id=at(dx=off, dp=-1), device_id_type=MESH)

    @pl.when(p < 3)
    def _():
        for off in range(4):
            pl.semaphore_signal(barrier, 1, device_id=at(dx=off, dp=1), device_id_type=MESH)

    sections = jnp.minimum(p, 1) + jnp.minimum(3 - p, 1)
    pl.semaphore_wait(barrier, len(peers) + 4 * sections)

    load_g.wait()
    tokens[2] = grads[picks_ref[3]]
    for m in range(3):
        chosen[pl.ds(m * rows, rows), :] = grads[picks_ref[m]]
    load_w.wait()

    def token_copy(off):
        return pltpu.make_async_remote_copy(
            src_ref=tokens.at[2],
            dst_ref=tokens.at[(2 + off) % 4],
            send_sem=token_send.at[off - 1],
            recv_sem=token_recv.at[off - 1],
            device_id=at(dx=off),
            device_id_type=MESH,
        )

    weight_copy = pltpu.make_async_remote_copy(
        src_ref=weights.at[0],
        dst_ref=weights.at[1],
        send_sem=weight_send,
        recv_sem=weight_recv,
        device_id=at(dz=1),
        device_id_type=MESH,
    )

    @pl.when(p > 0)
    def _():
        for off in (1, 2, 3):
            token_copy(off).start()
        weight_copy.start()

    def result_copy(j, b):
        zb = lax.rem(zh + b, 2)
        start = pl.multiple_of((zb * 4 + x) * block, block)
        return pltpu.make_async_remote_copy(
            src_ref=results.at[j, b],
            dst_ref=passed_hbm.at[:, pl.ds(start, block)],
            send_sem=result_send.at[j, b],
            recv_sem=result_recv.at[j, b],
            device_id=at(dx=(2 - j) % 4, dp=-1),
            device_id_type=MESH,
        )

    def section(b):
        for j in (2, 0, 1, 3):

            @pl.loop(0, block // 256)
            def _(n):
                col = pl.multiple_of(n * 256, 256)
                product = lax.dot_general(
                    tokens[j],
                    weights[b, pl.ds(col, 256), :],
                    (((1,), (1,)), ((), ())),
                    preferred_element_type=jnp.float32,
                )
                results[j, b, :, pl.ds(col, 256)] = product.astype(jnp.bfloat16)

            result_copy(j, b).start()

    def exponent(biggest):
        return jnp.floor(jnp.log2(jnp.maximum(biggest, 1e-30))) + 1.0

    def scale_of(packet):
        power = packet[0:LEAD, :].astype(jnp.int32).astype(jnp.float32)
        return jnp.exp2(power) * (1.0 / TOP)

    def pack(packet, biggest):
        power = exponent(biggest)
        packet[0:LEAD, :] = power.astype(jnp.int32).astype(jnp.int16)
        inverse = jnp.exp2(-power) * TOP

        @pl.loop(0, groups)
        def _(g):
            at_row = pl.multiple_of(g * LEAD, LEAD)
            to_row = pl.multiple_of(g * LEAD + LEAD, LEAD)
            value = jnp.round(wide[pl.ds(at_row, LEAD), :] * inverse)
            packet[pl.ds(to_row, LEAD), :] = value.astype(jnp.int32).astype(jnp.int16)

    def add_packets(sources, target):
        scales = [scale_of(s) for s in sources]

        def step(g, biggest):
            at_row = pl.multiple_of(g * LEAD, LEAD)
            from_row = pl.multiple_of(g * LEAD + LEAD, LEAD)
            total = None
            for s, scale in zip(sources, scales):
                term = s[pl.ds(from_row, LEAD), :].astype(jnp.int32).astype(jnp.float32) * scale
                total = term if total is None else total + term
            wide[pl.ds(at_row, LEAD), :] = total
            return jnp.maximum(biggest, jnp.abs(total))

        pack(target, lax.fori_loop(0, groups, step, jnp.zeros(scales[0].shape, jnp.float32)))

    def products(k, lo, hi):
        @pl.loop(lo * 2, hi * 2)
        def _(n):
            j = lax.div(n, 2)
            half = lax.rem(n, 2)
            piece = (half * 4 + wrap(x + 2 - k)) * 4 + wrap(y + 2 - j)
            source = cycle_ref[piece]
            left = jnp.concatenate(
                [acts[source, picks_ref[m]] for m in range(3)],
                axis=0,
            )
            value = lax.dot_general(
                left, chosen[...], (((0,), (0,)), ((), ())), preferred_element_type=jnp.float32
            )
            wide[...] = value
            biggest = jnp.max(jnp.abs(value.reshape(groups, LEAD, value.shape[1])), axis=0)
            pack(part.at[k, j, half], biggest)

    def one_copy(k, half):
        return pltpu.make_async_remote_copy(
            src_ref=part.at[k, 0, half],
            dst_ref=first_in.at[k, half],
            send_sem=one_send.at[0, k, half],
            recv_sem=one_recv.at[0, k, half],
            device_id=at(dy=3 if half else 1),
            device_id_type=MESH,
        )

    def pair_copy(k, side):
        return pltpu.make_async_remote_copy(
            src_ref=part.at[k, 3 if side else 1],
            dst_ref=first_pair.at[k, side],
            send_sem=pair_send.at[0, k, side],
            recv_sem=pair_recv.at[0, k, side],
            device_id=at(dy=3 if side else 1),
            device_id_type=MESH,
        )

    def compute(k):
        products(k, 0, 1)
        one_copy(k, 0).start()
        one_copy(k, 1).start()
        products(k, 1, 4)

    def relay(k):
        for half in (0, 1):
            one_copy(k, half).wait_recv()
            mine = part.at[k, 3 if half else 1, half]
            add_packets([mine, first_in.at[k, half]], mine)
            pair_copy(k, half).start()

    def settle(k):
        pair_copy(k, 0).wait_recv()
        pair_copy(k, 1).wait_recv()

        @pl.loop(0, 2)
        def _(half):
            mine = part.at[k, 2, half]
            add_packets([mine, first_pair.at[k, 0, half], first_pair.at[k, 1, half]], mine)

    def x_one(half):
        return pltpu.make_async_remote_copy(
            src_ref=part.at[0, 2, half],
            dst_ref=second_in.at[half],
            send_sem=one_send.at[1, 0, half],
            recv_sem=one_recv.at[1, 0, half],
            device_id=at(dx=3 if half else 1),
            device_id_type=MESH,
        )

    def x_pair(side):
        return pltpu.make_async_remote_copy(
            src_ref=part.at[3 if side else 1, 2],
            dst_ref=second_pair.at[side],
            send_sem=pair_send.at[1, 0, side],
            recv_sem=pair_recv.at[1, 0, side],
            device_id=at(dx=3 if side else 1),
            device_id_type=MESH,
        )

    def x_relay(side):
        x_one(side).wait_recv()
        mine = part.at[3 if side else 1, 2, side]
        add_packets([mine, second_in.at[side]], mine)
        x_pair(side).start()

    @pl.loop(0, acts.shape[0])
    def _(n):
        load_piece(n).wait()

    compute(0)

    @pl.when(p > 0)
    def _():
        for off in (1, 2, 3):
            token_copy(off).wait_recv()
        section(0)

    compute(1)
    relay(0)

    @pl.when(p > 0)
    def _():
        weight_copy.wait_recv()
        section(1)

    compute(3)
    relay(1)
    settle(0)
    x_one(0).start()
    x_one(1).start()
    compute(2)
    relay(3)
    settle(1)
    x_relay(0)
    relay(2)
    settle(3)
    x_relay(1)
    settle(2)
    x_pair(0).wait_recv()
    x_pair(1).wait_recv()

    other = 1 - zh
    add_packets(
        [part.at[2, 2, other], second_pair.at[0, other], second_pair.at[1, other]], z_out
    )
    z_copy = pltpu.make_async_remote_copy(
        src_ref=z_out,
        dst_ref=z_in,
        send_sem=z_send,
        recv_sem=z_recv,
        device_id=at(dz=1),
        device_id_type=MESH,
    )
    z_copy.start()
    mine = part.at[2, 2, zh]
    add_packets([mine, second_pair.at[0, zh], second_pair.at[1, zh]], mine)
    z_copy.wait_recv()
    add_packets([mine, z_in], last)

    def last_copy(off):
        return pltpu.make_async_remote_copy(
            src_ref=last,
            dst_ref=pieces_hbm.at[y],
            send_sem=last_send.at[off - 1],
            recv_sem=last_recv.at[off - 1],
            device_id=at(dy=off),
            device_id_type=MESH,
        )

    for off in (1, 2, 3):
        last_copy(off).start()
    keep = pltpu.make_async_copy(last, pieces_hbm.at[y], keep_sem)
    keep.start()

    for k in range(4):
        for half in (0, 1):
            one_copy(k, half).wait_send()
            pair_copy(k, half).wait_send()
    for half in (0, 1):
        x_one(half).wait_send()
        x_pair(half).wait_send()
    z_copy.wait_send()

    @pl.when(p > 0)
    def _():
        for off in (1, 2, 3):
            token_copy(off).wait_send()
        weight_copy.wait_send()
        for j in range(4):
            for b in (0, 1):
                result_copy(j, b).wait_send()

    @pl.when(p < 3)
    def _():
        for j in range(4):
            for b in (0, 1):
                result_copy(j, b).wait_recv()

    keep.wait()
    for off in (1, 2, 3):
        last_copy(off).wait()


def body(acts, key_grads, weights, b_slot, cycle):
    stored = acts[0, 0]
    key_store = key_grads[0, 0]
    weight_local = weights[0]
    micro, rows, features = stored.shape
    width = key_store.shape[2]
    block = weight_local.shape[0]
    piece_rows = features // cycle.shape[0]
    tall = piece_rows + LEAD
    place = jnp.arange(micro, dtype=jnp.int32)
    picks = jnp.where(place == micro - 1, b_slot, place + (place >= b_slot).astype(jnp.int32))
    dma = pltpu.SemaphoreType.DMA
    any_space = pl.BlockSpec(memory_space=pl.ANY)
    smem = pl.BlockSpec(memory_space=pltpu.SMEM)
    code = jnp.int16
    passed, pieces = pl.pallas_call(
        kernel,
        out_shape=(
            jax.ShapeDtypeStruct((rows, features), jnp.bfloat16),
            jax.ShapeDtypeStruct((4, tall, width), code),
        ),
        in_specs=[smem, smem, any_space, any_space, any_space],
        out_specs=(any_space, any_space),
        scratch_shapes=[
            pltpu.VMEM((cycle.shape[0], micro, rows, piece_rows), jnp.bfloat16),
            pltpu.VMEM(key_store.shape, jnp.bfloat16),
            pltpu.VMEM((2, block, width), jnp.bfloat16),
            pltpu.VMEM(((micro - 1) * rows, width), jnp.bfloat16),
            pltpu.VMEM((4, rows, width), jnp.bfloat16),
            pltpu.VMEM((4, 2, rows, block), jnp.bfloat16),
            pltpu.VMEM((4, 4, 2, tall, width), code),
            pltpu.VMEM((4, 2, tall, width), code),
            pltpu.VMEM((4, 2, 2, tall, width), code),
            pltpu.VMEM((2, tall, width), code),
            pltpu.VMEM((2, 2, tall, width), code),
            pltpu.VMEM((tall, width), code),
            pltpu.VMEM((tall, width), code),
            pltpu.VMEM((tall, width), code),
            pltpu.VMEM((piece_rows, width), jnp.float32),
            dma((2,)),
            dma((cycle.shape[0],)),
            dma((3,)),
            dma((3,)),
            dma,
            dma,
            dma((4, 2)),
            dma((4, 2)),
            dma((2, 4, 2)),
            dma((2, 4, 2)),
            dma((2, 4, 2)),
            dma((2, 4, 2)),
            dma,
            dma,
            dma((3,)),
            dma((3,)),
            dma,
        ],
        compiler_params=pltpu.CompilerParams(
            collective_id=0, has_side_effects=True, vmem_limit_bytes=60 * 1024 * 1024
        ),
        name="window",
    )(picks, cycle, stored, key_store, weight_local)
    passed = jnp.where(lax.axis_index("pipe") == 3, jnp.zeros((), passed.dtype), passed)
    scale = jnp.exp2(pieces[:, :LEAD].astype(jnp.float32)) * (1.0 / TOP)
    codes = pieces[:, LEAD:].astype(jnp.float32).reshape(4, piece_rows // LEAD, LEAD, width)
    owned = (codes * scale[:, None]).reshape(4 * piece_rows, width)
    return passed[None, None], owned[None]


def solution(mesh):
    placed = (
        P("dp", "pipe", None, "ctx", None),
        P("dp", "pipe", None, "ctx", None),
        P("pipe", "ctx", None),
        P("pipe"),
        P(),
    )
    return jax.shard_map(
        body,
        mesh=mesh,
        in_specs=placed,
        out_specs=(P("dp", "pipe", "ctx", None), P("pipe", "ctx", None)),
        check_vma=False,
    )
```

```python
import functools

import jax
import jax.numpy as jnp
from jax import lax
from jax.experimental import pallas as pl
from jax.experimental.pallas import tpu as pltpu
from jax.sharding import PartitionSpec as P

MESH = pl.DeviceIdType.MESH
TOP = 32700.0
LEAD = 16


def wrap(value):
    return lax.rem(value + 8, 4)


def kernel(
    picks_ref,
    cycle_ref,
    acts_hbm,
    grads_hbm,
    weights_hbm,
    passed_hbm,
    pieces_hbm,
    acts,
    grads,
    weights,
    chosen,
    current,
    tokens,
    results,
    part,
    first_in,
    first_pair,
    second_in,
    second_pair,
    z_in,
    z_out,
    last,
    wide,
    load_sem,
    piece_sem,
    token_send,
    token_recv,
    weight_send,
    weight_recv,
    result_send,
    result_recv,
    one_send,
    one_recv,
    pair_send,
    pair_recv,
    x_one_send,
    x_one_recv,
    x_pair_send,
    x_pair_recv,
    z_send,
    z_recv,
    last_send,
    last_recv,
    keep_sem,
):
    y = lax.axis_index("dp")
    p = lax.axis_index("pipe")
    c = lax.axis_index("ctx")
    zh = lax.div(c, 4)
    x = lax.rem(c, 4)
    piece_rows = wide.shape[0]
    rows = grads.shape[1]
    block = weights.shape[1]
    groups = piece_rows // LEAD
    parts, lanes = part.shape[0], part.shape[-1]

    def at(dy=0, dx=0, dz=0, dp=0):
        zz = lax.rem(zh + dz, 2)
        return (wrap(y + dy), p + dp, zz * 4 + wrap(x + dx))

    load_g = pltpu.make_async_copy(grads_hbm, grads, load_sem.at[0])

    def load_piece(n):
        start = pl.multiple_of(n * piece_rows, piece_rows)
        return pltpu.make_async_copy(
            acts_hbm.at[:, :, pl.ds(start, piece_rows)], acts.at[n], piece_sem.at[n]
        )

    load_g.start()

    @pl.loop(0, acts.shape[0])
    def _(n):
        load_piece(n).start()


    barrier = pltpu.get_barrier_semaphore()
    peers = [at(dy=1), at(dy=2), at(dy=3), at(dx=1), at(dx=2), at(dx=3), at(dz=1)]
    for peer in peers:
        pl.semaphore_signal(barrier, 1, device_id=peer, device_id_type=MESH)

    @pl.when(p > 0)
    def _():
        for off in range(4):
            pl.semaphore_signal(barrier, 1, device_id=at(dx=off, dp=-1), device_id_type=MESH)
        pl.semaphore_signal(barrier, 1, device_id=at(dz=1, dp=-1), device_id_type=MESH)

    @pl.when(p < 3)
    def _():
        for off in range(4):
            pl.semaphore_signal(barrier, 1, device_id=at(dx=off, dp=1), device_id_type=MESH)
        pl.semaphore_signal(barrier, 1, device_id=at(dz=1, dp=1), device_id_type=MESH)

    sections = jnp.minimum(p, 1) + jnp.minimum(3 - p, 1)
    pl.semaphore_wait(barrier, len(peers) + 5 * sections)

    load_g.wait()
    current[...] = grads[picks_ref[3]]
    for m in range(3):
        chosen[pl.ds(m * rows, rows), :] = grads[picks_ref[m]]

    def token_copy(off):
        return pltpu.make_async_remote_copy(
            src_ref=current,
            dst_ref=tokens.at[(2 + off) % 4],
            send_sem=token_send.at[off],
            recv_sem=token_recv.at[off],
            device_id=at(dx=off, dp=-1),
            device_id_type=MESH,
        )

    def weight_copy(b):
        return pltpu.make_async_remote_copy(
            src_ref=weights_hbm,
            dst_ref=weights.at[b],
            send_sem=weight_send.at[b],
            recv_sem=weight_recv.at[b],
            device_id=at(dz=b, dp=-1),
            device_id_type=MESH,
        )

    @pl.when(p > 0)
    def _():
        for off in range(4):
            token_copy(off).start()
        weight_copy(0).start()
        weight_copy(1).start()

    def result_place(b):
        zb = lax.rem(zh + b, 2)
        return passed_hbm.at[:, pl.ds(pl.multiple_of((zb * 4 + x) * block, block), block)]

    def result_copy(j, b):
        return pltpu.make_async_remote_copy(
            src_ref=results.at[j, b],
            dst_ref=result_place(b),
            send_sem=result_send.at[j, b],
            recv_sem=result_recv.at[j, b],
            device_id=at(dx=(2 - j) % 4),
            device_id_type=MESH,
        )

    def result_keep(b):
        return pltpu.make_async_copy(results.at[2, b], result_place(b), result_send.at[2, b])

    def section(b):
        for j in (0, 1, 3, 2):

            @pl.loop(0, block // 256)
            def _(n):
                col = pl.multiple_of(n * 256, 256)
                product = lax.dot_general(
                    tokens[j],
                    weights[b, pl.ds(col, 256), :],
                    (((1,), (1,)), ((), ())),
                    preferred_element_type=jnp.float32,
                )
                results[j, b, :, pl.ds(col, 256)] = product.astype(jnp.bfloat16)

            if j == 2:
                result_keep(b).start()
            else:
                result_copy(j, b).start()

    def pack(packet, value):
        biggest = jnp.max(jnp.abs(value), axis=0)
        power = jnp.floor(jnp.log2(jnp.maximum(biggest, 1e-30))) + 1.0
        packet[0:LEAD, :] = power.astype(jnp.int32).astype(jnp.int16)
        codes = jnp.round(value * (jnp.exp2(-power) * TOP)[None])
        codes = codes.reshape(piece_rows, lanes).astype(jnp.int32)
        packet[LEAD:, :] = codes.astype(jnp.int16)

    def unpack(packet):
        power = packet[0:LEAD, :].astype(jnp.int32).astype(jnp.float32)
        codes = packet[LEAD:, :].astype(jnp.int32).astype(jnp.float32)
        return codes.reshape(groups, LEAD, lanes) * (jnp.exp2(power) * (1.0 / TOP))[None]

    def add_packets(sources, target):
        total = unpack(sources[0])
        for source in sources[1:]:
            total = total + unpack(source)
        pack(target, total)

    def products(k, lo, hi):
        @pl.loop(lo * 2, hi * 2)
        def _(n):
            j = lax.div(n, 2)
            half = lax.rem(n, 2)
            piece = (half * 4 + wrap(x + 2 - k)) * 4 + wrap(y + 2 - j)
            source = cycle_ref[piece]
            left = jnp.concatenate(
                [acts[source, picks_ref[m]] for m in range(3)],
                axis=0,
            )
            value = lax.dot_general(
                left, chosen[...], (((0,), (0,)), ((), ())), preferred_element_type=jnp.float32
            )
            wide[...] = value
            for q in range(parts):
                columns = wide[:, q * lanes : (q + 1) * lanes]
                pack(part.at[q, k, j, half], columns.reshape(groups, LEAD, lanes))

    def one_copy(k, half):
        return pltpu.make_async_remote_copy(
            src_ref=part.at[:, k, 0, half],
            dst_ref=first_in.at[k, half],
            send_sem=one_send.at[k, half],
            recv_sem=one_recv.at[k, half],
            device_id=at(dy=3 if half else 1),
            device_id_type=MESH,
        )

    def pair_copy(q, k, side):
        return pltpu.make_async_remote_copy(
            src_ref=part.at[q, k, 3 if side else 1],
            dst_ref=first_pair.at[q, k, side],
            send_sem=pair_send.at[q, k, side],
            recv_sem=pair_recv.at[q, k, side],
            device_id=at(dy=3 if side else 1),
            device_id_type=MESH,
        )

    def compute(k):
        products(k, 0, 1)
        one_copy(k, 0).start()
        one_copy(k, 1).start()
        products(k, 1, 4)

    def relay(q, k):
        for half in (0, 1):
            mine = part.at[q, k, 3 if half else 1, half]
            add_packets([mine, first_in.at[k, half, q]], mine)
            pair_copy(q, k, half).start()

    def settle(q, k):
        pair_copy(q, k, 0).wait_recv()
        pair_copy(q, k, 1).wait_recv()

        @pl.loop(0, 2)
        def _(half):
            mine = part.at[q, k, 2, half]
            add_packets([mine, first_pair.at[q, k, 0, half], first_pair.at[q, k, 1, half]], mine)

    def x_one(q, half):
        return pltpu.make_async_remote_copy(
            src_ref=part.at[q, 0, 2, half],
            dst_ref=second_in.at[q, half],
            send_sem=x_one_send.at[q, half],
            recv_sem=x_one_recv.at[q, half],
            device_id=at(dx=3 if half else 1),
            device_id_type=MESH,
        )

    def x_pair(q, side):
        return pltpu.make_async_remote_copy(
            src_ref=part.at[q, 3 if side else 1, 2],
            dst_ref=second_pair.at[q, side],
            send_sem=x_pair_send.at[q, side],
            recv_sem=x_pair_recv.at[q, side],
            device_id=at(dx=3 if side else 1),
            device_id_type=MESH,
        )

    def x_relay(q, side):
        x_one(q, side).wait_recv()
        mine = part.at[q, 3 if side else 1, 2, side]
        add_packets([mine, second_in.at[q, side]], mine)
        x_pair(q, side).start()

    def z_copy(q):
        return pltpu.make_async_remote_copy(
            src_ref=z_out.at[q],
            dst_ref=z_in.at[q],
            send_sem=z_send.at[q],
            recv_sem=z_recv.at[q],
            device_id=at(dz=1),
            device_id_type=MESH,
        )

    def x_final(q):
        x_pair(q, 0).wait_recv()
        x_pair(q, 1).wait_recv()
        other = 1 - zh

        def sources(half):
            return [
                part.at[q, 2, 2, half],
                second_pair.at[q, 0, half],
                second_pair.at[q, 1, half],
            ]

        add_packets(sources(other), z_out.at[q])
        z_copy(q).start()
        add_packets(sources(zh), part.at[q, 2, 2, zh])

    def place(q):
        return pieces_hbm.at[y, :, pl.ds(pl.multiple_of(q * lanes, lanes), lanes)]

    def last_copy(q, off):
        return pltpu.make_async_remote_copy(
            src_ref=last.at[q],
            dst_ref=place(q),
            send_sem=last_send.at[q, off - 1],
            recv_sem=last_recv.at[q, off - 1],
            device_id=at(dy=off),
            device_id_type=MESH,
        )

    def keep_copy(q):
        return pltpu.make_async_copy(last.at[q], place(q), keep_sem.at[q])

    def z_final(q):
        z_copy(q).wait_recv()
        add_packets([part.at[q, 2, 2, zh], z_in.at[q]], last.at[q])
        for off in (1, 2, 3):
            last_copy(q, off).start()
        keep_copy(q).start()

    @pl.loop(0, acts.shape[0])
    def _(n):
        load_piece(n).wait()

    compute(0)

    def one_wait(k):
        one_copy(k, 0).wait_recv()
        one_copy(k, 1).wait_recv()

    def relays(k):
        one_wait(k)

        @pl.loop(0, parts)
        def _(q):
            relay(q, k)

    compute(1)
    relays(0)

    @pl.when(p < 3)
    def _():
        for off in range(4):
            token_copy(off).wait_recv()
        weight_copy(0).wait_recv()
        section(0)


    compute(3)
    relays(1)

    @pl.when(p < 3)
    def _():
        weight_copy(1).wait_recv()
        section(1)

    compute(2)
    relays(3)

    @pl.loop(0, parts)
    def _(q):
        settle(q, 0)
        x_one(q, 0).start()
        x_one(q, 1).start()

    relays(2)

    @pl.loop(0, parts)
    def _(q):
        settle(q, 1)

    @pl.loop(0, parts)
    def _(q):
        settle(q, 3)
        x_relay(q, 0)
        x_relay(q, 1)

    @pl.loop(0, parts)
    def _(q):
        settle(q, 2)
        x_final(q)

        @pl.when(q > 0)
        def _():
            z_final(q - 1)

    z_final(parts - 1)

    for k in range(4):
        one_copy(k, 0).wait_send()
        one_copy(k, 1).wait_send()

    @pl.loop(0, parts)
    def _(q):
        for side in (0, 1):
            for k in range(4):
                pair_copy(q, k, side).wait_send()
            x_one(q, side).wait_send()
            x_pair(q, side).wait_send()
        z_copy(q).wait_send()

    @pl.when(p > 0)
    def _():
        for off in range(4):
            token_copy(off).wait_send()
        weight_copy(0).wait_send()
        weight_copy(1).wait_send()

    @pl.when(p < 3)
    def _():
        for b in (0, 1):
            for j in (0, 1, 3):
                result_copy(j, b).wait()
            result_keep(b).wait()

    @pl.loop(0, parts)
    def _(q):
        keep_copy(q).wait()
        for off in (1, 2, 3):
            last_copy(q, off).wait()


def finish(passed_in, pieces, passed, owned):
    groups = owned.shape[0] // LEAD
    power = pieces[0, 0:LEAD, :].astype(jnp.int32).astype(jnp.float32)
    scale = jnp.exp2(power) * (1.0 / TOP)

    @pl.loop(0, groups)
    def _(g):
        from_row = pl.multiple_of(g * LEAD + LEAD, LEAD)
        to_row = pl.multiple_of(g * LEAD, LEAD)
        codes = pieces[0, pl.ds(from_row, LEAD), :].astype(jnp.int32).astype(jnp.float32)
        owned[pl.ds(to_row, LEAD), :] = codes * scale

    last_section = lax.axis_index("pipe") == 3

    @pl.when(last_section)
    def _():
        passed[...] = jnp.zeros_like(passed)

    @pl.when(jnp.logical_not(last_section))
    def _():
        passed[...] = passed_in[...]


def body(acts, key_grads, weights, b_slot, cycle):
    stored = acts[0, 0]
    key_store = key_grads[0, 0]
    weight_local = weights[0]
    micro, rows, features = stored.shape
    width = key_store.shape[2]
    block = weight_local.shape[0]
    piece_rows = features // cycle.shape[0]
    tall = piece_rows + LEAD
    lanes = 128
    parts = width // lanes
    place = jnp.arange(micro, dtype=jnp.int32)
    picks = jnp.where(place == micro - 1, b_slot, place + (place >= b_slot).astype(jnp.int32))
    dma = pltpu.SemaphoreType.DMA
    any_space = pl.BlockSpec(memory_space=pl.ANY)
    smem = pl.BlockSpec(memory_space=pltpu.SMEM)
    code = jnp.int16
    passed, pieces = pl.pallas_call(
        kernel,
        out_shape=(
            jax.ShapeDtypeStruct((rows, features), jnp.bfloat16),
            jax.ShapeDtypeStruct((4, tall, width), code),
        ),
        in_specs=[smem, smem, any_space, any_space, any_space],
        out_specs=(any_space, any_space),
        scratch_shapes=[
            pltpu.VMEM((cycle.shape[0], micro, rows, piece_rows), jnp.bfloat16),
            pltpu.VMEM(key_store.shape, jnp.bfloat16),
            pltpu.VMEM((2, block, width), jnp.bfloat16),
            pltpu.VMEM(((micro - 1) * rows, width), jnp.bfloat16),
            pltpu.VMEM((rows, width), jnp.bfloat16),
            pltpu.VMEM((4, rows, width), jnp.bfloat16),
            pltpu.VMEM((4, 2, rows, block), jnp.bfloat16),
            pltpu.VMEM((parts, 4, 4, 2, tall, lanes), code),
            pltpu.VMEM((4, 2, parts, tall, lanes), code),
            pltpu.VMEM((parts, 4, 2, 2, tall, lanes), code),
            pltpu.VMEM((parts, 2, tall, lanes), code),
            pltpu.VMEM((parts, 2, 2, tall, lanes), code),
            pltpu.VMEM((parts, tall, lanes), code),
            pltpu.VMEM((parts, tall, lanes), code),
            pltpu.VMEM((parts, tall, lanes), code),
            pltpu.VMEM((piece_rows, width), jnp.float32),
            dma((1,)),
            dma((cycle.shape[0],)),
            dma((4,)),
            dma((4,)),
            dma((2,)),
            dma((2,)),
            dma((4, 2)),
            dma((4, 2)),
            dma((4, 2)),
            dma((4, 2)),
            dma((parts, 4, 2)),
            dma((parts, 4, 2)),
            dma((parts, 2)),
            dma((parts, 2)),
            dma((parts, 2)),
            dma((parts, 2)),
            dma((parts,)),
            dma((parts,)),
            dma((parts, 3)),
            dma((parts, 3)),
            dma((parts,)),
        ],
        compiler_params=pltpu.CompilerParams(
            collective_id=0, has_side_effects=True, vmem_limit_bytes=60 * 1024 * 1024
        ),
        name="window",
    )(picks, cycle, stored, key_store, weight_local)
    wide_block = pl.BlockSpec((rows, features // 4), lambda n: (0, n))
    passed, owned = pl.pallas_call(
        finish,
        grid=(4,),
        out_shape=(
            jax.ShapeDtypeStruct(passed.shape, passed.dtype),
            jax.ShapeDtypeStruct((4 * piece_rows, width), jnp.float32),
        ),
        in_specs=[wide_block, pl.BlockSpec((1, tall, width), lambda n: (n, 0, 0))],
        out_specs=(wide_block, pl.BlockSpec((piece_rows, width), lambda n: (n, 0))),
        compiler_params=pltpu.CompilerParams(vmem_limit_bytes=60 * 1024 * 1024),
        name="finish",
    )(passed, pieces)
    return passed[None, None], owned[None]


def solution(mesh):
    placed = (
        P("dp", "pipe", None, "ctx", None),
        P("dp", "pipe", None, "ctx", None),
        P("pipe", "ctx", None),
        P("pipe"),
        P(),
    )
    return jax.shard_map(
        body,
        mesh=mesh,
        in_specs=placed,
        out_specs=(P("dp", "pipe", "ctx", None), P("pipe", "ctx", None)),
        check_vma=False,
    )
```

```python
import functools

import jax
import jax.numpy as jnp
from jax import lax
from jax.experimental import pallas as pl
from jax.experimental.pallas import tpu as pltpu
from jax.sharding import PartitionSpec as P

MESH = pl.DeviceIdType.MESH
TOP = 32700.0
LEAD = 16


def wrap(value):
    return lax.rem(value + 8, 4)


def kernel(
    picks_ref,
    cycle_ref,
    acts_hbm,
    grads_hbm,
    weights_hbm,
    passed_hbm,
    pieces_hbm,
    acts,
    grads,
    weights,
    chosen,
    current,
    tokens,
    results,
    part,
    first_in,
    first_pair,
    x_in,
    z_in,
    last,
    over_in,
    late_in,
    late_pair_in,
    late_x_in,
    wide,
    load_sem,
    piece_sem,
    token_send,
    token_recv,
    weight_send,
    weight_recv,
    result_send,
    result_recv,
    one_send,
    one_recv,
    pair_send,
    pair_recv,
    x_send,
    x_recv,
    z_send,
    z_recv,
    last_send,
    last_recv,
    keep_sem,
    over_send,
    over_recv,
    late_one_send,
    late_one_recv,
    late_pair_send,
    late_pair_recv,
    late_x_send,
    late_x_recv,
):
    y = lax.axis_index("dp")
    p = lax.axis_index("pipe")
    c = lax.axis_index("ctx")
    zh = lax.div(c, 4)
    x = lax.rem(c, 4)
    piece_rows = wide.shape[0]
    rows = grads.shape[1]
    block = weights.shape[1]
    groups = piece_rows // LEAD
    parts, lanes = part.shape[0], part.shape[-1]
    early = parts - 1

    def at(dy=0, dx=0, dz=0, dp=0):
        zz = lax.rem(zh + dz, 2)
        return (wrap(y + dy), p + dp, zz * 4 + wrap(x + dx))

    load_g = pltpu.make_async_copy(grads_hbm, grads, load_sem.at[0])

    def load_piece(n):
        start = pl.multiple_of(n * piece_rows, piece_rows)
        return pltpu.make_async_copy(
            acts_hbm.at[:, :, pl.ds(start, piece_rows)], acts.at[n], piece_sem.at[n]
        )

    load_g.start()

    @pl.loop(0, acts.shape[0])
    def _(n):
        load_piece(n).start()


    barrier = pltpu.get_barrier_semaphore()
    peers = [at(dy=1), at(dy=2), at(dy=3), at(dx=1), at(dx=2), at(dx=3), at(dz=1)]
    for peer in peers:
        pl.semaphore_signal(barrier, 1, device_id=peer, device_id_type=MESH)

    @pl.when(p > 0)
    def _():
        for off in range(4):
            pl.semaphore_signal(barrier, 1, device_id=at(dx=off, dp=-1), device_id_type=MESH)
        pl.semaphore_signal(barrier, 1, device_id=at(dz=1, dp=-1), device_id_type=MESH)

    @pl.when(p < 3)
    def _():
        for off in range(4):
            pl.semaphore_signal(barrier, 1, device_id=at(dx=off, dp=1), device_id_type=MESH)
        pl.semaphore_signal(barrier, 1, device_id=at(dz=1, dp=1), device_id_type=MESH)

    sections = jnp.minimum(p, 1) + jnp.minimum(3 - p, 1)
    pl.semaphore_wait(barrier, len(peers) + 5 * sections)

    def weight_copy(b):
        return pltpu.make_async_remote_copy(
            src_ref=weights_hbm,
            dst_ref=weights.at[b],
            send_sem=weight_send.at[b],
            recv_sem=weight_recv.at[b],
            device_id=at(dz=b, dp=-1),
            device_id_type=MESH,
        )

    @pl.when(p > 0)
    def _():
        weight_copy(0).start()
        weight_copy(1).start()

    load_g.wait()
    current[...] = grads[picks_ref[3]]
    for m in range(3):
        chosen[pl.ds(m * rows, rows), :] = grads[picks_ref[m]]

    def token_copy(off):
        return pltpu.make_async_remote_copy(
            src_ref=current,
            dst_ref=tokens.at[(2 + off) % 4],
            send_sem=token_send.at[off],
            recv_sem=token_recv.at[off],
            device_id=at(dx=off, dp=-1),
            device_id_type=MESH,
        )

    @pl.when(p > 0)
    def _():
        for off in range(4):
            token_copy(off).start()

    def result_place(b):
        zb = lax.rem(zh + b, 2)
        return passed_hbm.at[:, pl.ds(pl.multiple_of((zb * 4 + x) * block, block), block)]

    def result_copy(j, b):
        return pltpu.make_async_remote_copy(
            src_ref=results.at[j, b],
            dst_ref=result_place(b),
            send_sem=result_send.at[j, b],
            recv_sem=result_recv.at[j, b],
            device_id=at(dx=(2 - j) % 4),
            device_id_type=MESH,
        )

    def result_keep(b):
        return pltpu.make_async_copy(results.at[2, b], result_place(b), result_send.at[2, b])

    def section(b):
        for j in (0, 1, 3, 2):

            @pl.loop(0, block // 256)
            def _(n):
                col = pl.multiple_of(n * 256, 256)
                product = lax.dot_general(
                    tokens[j],
                    weights[b, pl.ds(col, 256), :],
                    (((1,), (1,)), ((), ())),
                    preferred_element_type=jnp.float32,
                )
                results[j, b, :, pl.ds(col, 256)] = product.astype(jnp.bfloat16)

            if j == 2:
                result_keep(b).start()
            else:
                result_copy(j, b).start()

    def pack(packet, value):
        biggest = jnp.max(jnp.abs(value), axis=0)
        power = jnp.floor(jnp.log2(jnp.maximum(biggest, 1e-30))) + 1.0
        packet[0:LEAD, :] = power.astype(jnp.int32).astype(jnp.int16)
        codes = jnp.round(value * (jnp.exp2(-power) * TOP)[None])
        codes = codes.reshape(piece_rows, lanes).astype(jnp.int32)
        packet[LEAD:, :] = codes.astype(jnp.int16)

    def unpack(packet):
        power = packet[0:LEAD, :].astype(jnp.int32).astype(jnp.float32)
        codes = packet[LEAD:, :].astype(jnp.int32).astype(jnp.float32)
        return codes.reshape(groups, LEAD, lanes) * (jnp.exp2(power) * (1.0 / TOP))[None]

    def add_packets(sources, target):
        total = unpack(sources[0])
        for source in sources[1:]:
            total = total + unpack(source)
        pack(target, total)

    def products(k, lo, hi):
        @pl.loop(lo * 2, hi * 2)
        def _(n):
            j = lax.div(n, 2)
            half = lax.rem(n, 2)
            piece = (half * 4 + wrap(x + 2 - k)) * 4 + wrap(y + 2 - j)
            source = cycle_ref[piece]
            left = jnp.concatenate(
                [acts[source, picks_ref[m]] for m in range(3)],
                axis=0,
            )
            value = lax.dot_general(
                left, chosen[...], (((0,), (0,)), ((), ())), preferred_element_type=jnp.float32
            )
            wide[...] = value
            for q in range(parts):
                columns = wide[:, q * lanes : (q + 1) * lanes]
                pack(part.at[q, k, j, half], columns.reshape(groups, LEAD, lanes))

    def one_copy(k, half):
        return pltpu.make_async_remote_copy(
            src_ref=part.at[pl.ds(0, early), k, 0, half],
            dst_ref=first_in.at[k, half],
            send_sem=one_send.at[k, half],
            recv_sem=one_recv.at[k, half],
            device_id=at(dy=3 if half else 1),
            device_id_type=MESH,
        )

    def pair_copy(q, k, side):
        return pltpu.make_async_remote_copy(
            src_ref=part.at[q, k, 3 if side else 1],
            dst_ref=first_pair.at[q, k, side],
            send_sem=pair_send.at[q, k, side],
            recv_sem=pair_recv.at[q, k, side],
            device_id=at(dy=3 if side else 1),
            device_id_type=MESH,
        )

    def over_copy(k):
        return pltpu.make_async_remote_copy(
            src_ref=part.at[early, k, :, 1 - zh],
            dst_ref=over_in.at[k],
            send_sem=over_send.at[k],
            recv_sem=over_recv.at[k],
            device_id=at(dz=1),
            device_id_type=MESH,
        )

    def over_add(k):
        over_copy(k).wait_recv()

        @pl.loop(0, 4)
        def _(j):
            mine = part.at[early, k, j, zh]
            add_packets([mine, over_in.at[k, j]], mine)

    def late_one(side):
        return pltpu.make_async_remote_copy(
            src_ref=part.at[early, pl.ds(2 * side, 2), 0, zh],
            dst_ref=late_in.at[side],
            send_sem=late_one_send.at[side],
            recv_sem=late_one_recv.at[side],
            device_id=at(dy=3 if side else 1),
            device_id_type=MESH,
        )

    def late_pair(side, lot):
        return pltpu.make_async_remote_copy(
            src_ref=part.at[early, pl.ds(2 * lot, 2), 3 if side else 1, zh],
            dst_ref=late_pair_in.at[side, lot],
            send_sem=late_pair_send.at[side, lot],
            recv_sem=late_pair_recv.at[side, lot],
            device_id=at(dy=3 if side else 1),
            device_id_type=MESH,
        )

    def late_relay(side):
        late_one(side).wait_recv()

        @pl.loop(0, 2)
        def _(n):
            mine = part.at[early, 2 * side + n, 3 if side else 1, zh]
            add_packets([mine, late_in.at[side, n]], mine)

        late_pair(side, side).start()

    def late_x(k):
        return pltpu.make_async_remote_copy(
            src_ref=part.at[early, k, 2, zh],
            dst_ref=late_x_in.at[k],
            send_sem=late_x_send.at[k],
            recv_sem=late_x_recv.at[k],
            device_id=at(dx=(2 - k) % 4),
            device_id_type=MESH,
        )

    def late_settle():
        for side in (0, 1):
            for lot in (0, 1):
                late_pair(side, lot).wait_recv()

        @pl.loop(0, 4)
        def _(k):
            lot = lax.div(k, 2)
            n = lax.rem(k, 2)
            mine = part.at[early, k, 2, zh]
            add_packets([mine, late_pair_in.at[0, lot, n], late_pair_in.at[1, lot, n]], mine)

        for k in (0, 1, 3):
            late_x(k).start()

    def late_final():
        for k in (0, 1, 3):
            late_x(k).wait_recv()
        add_packets(
            [part.at[early, 2, 2, zh], late_x_in.at[0], late_x_in.at[1], late_x_in.at[3]],
            last.at[early],
        )
        share(early)

    def compute(k):
        products(k, 0, 1)
        one_copy(k, 0).start()
        one_copy(k, 1).start()
        products(k, 1, 4)

    def relay(q, k):
        for half in (0, 1):
            mine = part.at[q, k, 3 if half else 1, half]
            add_packets([mine, first_in.at[k, half, q]], mine)
            pair_copy(q, k, half).start()

    def settle(q, k):
        pair_copy(q, k, 0).wait_recv()
        pair_copy(q, k, 1).wait_recv()

        @pl.loop(0, 2)
        def _(half):
            mine = part.at[q, k, 2, half]
            add_packets([mine, first_pair.at[q, k, 0, half], first_pair.at[q, k, 1, half]], mine)

    def z_copy(q, k):
        return pltpu.make_async_remote_copy(
            src_ref=part.at[q, k, 2, 1 - zh],
            dst_ref=z_in.at[q, k],
            send_sem=z_send.at[q, k],
            recv_sem=z_recv.at[q, k],
            device_id=at(dz=1),
            device_id_type=MESH,
        )

    def x_copy(q, k):
        return pltpu.make_async_remote_copy(
            src_ref=part.at[q, k, 2, zh],
            dst_ref=x_in.at[q, k],
            send_sem=x_send.at[q, k],
            recv_sem=x_recv.at[q, k],
            device_id=at(dx=(2 - k) % 4),
            device_id_type=MESH,
        )

    def z_add(q, k):
        z_copy(q, k).wait_recv()
        mine = part.at[q, k, 2, zh]
        add_packets([mine, z_in.at[q, k]], mine)
        x_copy(q, k).start()

    def place(q):
        return pieces_hbm.at[y, :, pl.ds(pl.multiple_of(q * lanes, lanes), lanes)]

    def last_copy(q, off):
        return pltpu.make_async_remote_copy(
            src_ref=last.at[q],
            dst_ref=place(q),
            send_sem=last_send.at[q, off - 1],
            recv_sem=last_recv.at[q, off - 1],
            device_id=at(dy=off),
            device_id_type=MESH,
        )

    def keep_copy(q):
        return pltpu.make_async_copy(last.at[q], place(q), keep_sem.at[q])

    def share(q):
        for off in (1, 2, 3):
            last_copy(q, off).start()
        keep_copy(q).start()

    def final(q):
        z_copy(q, 2).wait_recv()
        for k in (0, 1, 3):
            x_copy(q, k).wait_recv()
        add_packets(
            [part.at[q, 2, 2, zh], z_in.at[q, 2], x_in.at[q, 0], x_in.at[q, 1], x_in.at[q, 3]],
            last.at[q],
        )
        share(q)

    @pl.loop(0, acts.shape[0])
    def _(n):
        load_piece(n).wait()

    compute(0)

    def one_wait(k):
        one_copy(k, 0).wait_recv()
        one_copy(k, 1).wait_recv()

    def relays(k):
        one_wait(k)

        @pl.loop(0, early)
        def _(q):
            relay(q, k)

    compute(1)
    relays(0)

    @pl.when(p < 3)
    def _():
        for off in range(4):
            token_copy(off).wait_recv()
        weight_copy(0).wait_recv()
        section(0)

    compute(3)
    relays(1)

    over_copy(0).start()
    over_copy(1).start()
    over_copy(3).start()
    compute(2)
    over_copy(2).start()

    @pl.when(p < 3)
    def _():
        weight_copy(1).wait_recv()
        section(1)

    relays(3)

    relays(2)

    @pl.loop(0, early)
    def _(q):
        settle(q, 0)
        z_copy(q, 0).start()

    @pl.loop(0, early)
    def _(q):
        settle(q, 1)
        z_copy(q, 1).start()
        z_add(q, 0)

    over_add(0)
    over_add(1)
    late_one(0).start()
    over_add(3)
    over_add(2)
    late_one(1).start()
    late_pair(0, 1).start()
    late_pair(1, 0).start()

    @pl.loop(0, early)
    def _(q):
        settle(q, 3)
        z_copy(q, 3).start()
        z_add(q, 1)

    late_relay(0)
    late_relay(1)

    @pl.loop(0, early)
    def _(q):
        settle(q, 2)
        z_copy(q, 2).start()
        z_add(q, 3)

        @pl.when(q == early - 1)
        def _():
            late_settle()

        @pl.when(q > 0)
        def _():
            final(q - 1)

    late_final()
    final(early - 1)

    for k in range(4):
        one_copy(k, 0).wait_send()
        one_copy(k, 1).wait_send()

        over_copy(k).wait_send()
    for side in (0, 1):
        late_one(side).wait_send()
        late_pair(side, 0).wait_send()
        late_pair(side, 1).wait_send()
    for k in (0, 1, 3):
        late_x(k).wait_send()

    @pl.loop(0, early)
    def _(q):
        for side in (0, 1):
            for k in range(4):
                pair_copy(q, k, side).wait_send()
        for k in (0, 1, 3):
            x_copy(q, k).wait_send()
        for k in range(4):
            z_copy(q, k).wait_send()

    @pl.when(p > 0)
    def _():
        for off in range(4):
            token_copy(off).wait_send()
        weight_copy(0).wait_send()
        weight_copy(1).wait_send()

    @pl.when(p < 3)
    def _():
        for b in (0, 1):
            for j in (0, 1, 3):
                result_copy(j, b).wait()
            result_keep(b).wait()

    @pl.loop(0, parts)
    def _(q):
        keep_copy(q).wait()
        for off in (1, 2, 3):
            last_copy(q, off).wait()


def finish(passed_in, pieces, passed, owned):
    groups = owned.shape[0] // LEAD
    power = pieces[0, 0:LEAD, :].astype(jnp.int32).astype(jnp.float32)
    scale = jnp.exp2(power) * (1.0 / TOP)

    @pl.loop(0, groups)
    def _(g):
        from_row = pl.multiple_of(g * LEAD + LEAD, LEAD)
        to_row = pl.multiple_of(g * LEAD, LEAD)
        codes = pieces[0, pl.ds(from_row, LEAD), :].astype(jnp.int32).astype(jnp.float32)
        owned[pl.ds(to_row, LEAD), :] = codes * scale

    last_section = lax.axis_index("pipe") == 3

    @pl.when(last_section)
    def _():
        passed[...] = jnp.zeros_like(passed)

    @pl.when(jnp.logical_not(last_section))
    def _():
        passed[...] = passed_in[...]


def body(acts, key_grads, weights, b_slot, cycle):
    stored = acts[0, 0]
    key_store = key_grads[0, 0]
    weight_local = weights[0]
    micro, rows, features = stored.shape
    width = key_store.shape[2]
    block = weight_local.shape[0]
    piece_rows = features // cycle.shape[0]
    tall = piece_rows + LEAD
    lanes = 128
    parts = width // lanes
    early = parts - 1
    place = jnp.arange(micro, dtype=jnp.int32)
    picks = jnp.where(place == micro - 1, b_slot, place + (place >= b_slot).astype(jnp.int32))
    dma = pltpu.SemaphoreType.DMA
    any_space = pl.BlockSpec(memory_space=pl.ANY)
    smem = pl.BlockSpec(memory_space=pltpu.SMEM)
    code = jnp.int16
    passed, pieces = pl.pallas_call(
        kernel,
        out_shape=(
            jax.ShapeDtypeStruct((rows, features), jnp.bfloat16),
            jax.ShapeDtypeStruct((4, tall, width), code),
        ),
        in_specs=[smem, smem, any_space, any_space, any_space],
        out_specs=(any_space, any_space),
        scratch_shapes=[
            pltpu.VMEM((cycle.shape[0], micro, rows, piece_rows), jnp.bfloat16),
            pltpu.VMEM(key_store.shape, jnp.bfloat16),
            pltpu.VMEM((2, block, width), jnp.bfloat16),
            pltpu.VMEM(((micro - 1) * rows, width), jnp.bfloat16),
            pltpu.VMEM((rows, width), jnp.bfloat16),
            pltpu.VMEM((4, rows, width), jnp.bfloat16),
            pltpu.VMEM((4, 2, rows, block), jnp.bfloat16),
            pltpu.VMEM((parts, 4, 4, 2, tall, lanes), code),
            pltpu.VMEM((4, 2, early, tall, lanes), code),
            pltpu.VMEM((early, 4, 2, 2, tall, lanes), code),
            pltpu.VMEM((early, 4, tall, lanes), code),
            pltpu.VMEM((early, 4, tall, lanes), code),
            pltpu.VMEM((parts, tall, lanes), code),
            pltpu.VMEM((4, 4, tall, lanes), code),
            pltpu.VMEM((2, 2, tall, lanes), code),
            pltpu.VMEM((2, 2, 2, tall, lanes), code),
            pltpu.VMEM((4, tall, lanes), code),
            pltpu.VMEM((piece_rows, width), jnp.float32),
            dma((1,)),
            dma((cycle.shape[0],)),
            dma((4,)),
            dma((4,)),
            dma((2,)),
            dma((2,)),
            dma((4, 2)),
            dma((4, 2)),
            dma((4, 2)),
            dma((4, 2)),
            dma((early, 4, 2)),
            dma((early, 4, 2)),
            dma((early, 4)),
            dma((early, 4)),
            dma((early, 4)),
            dma((early, 4)),
            dma((parts, 3)),
            dma((parts, 3)),
            dma((parts,)),
            dma((4,)),
            dma((4,)),
            dma((2,)),
            dma((2,)),
            dma((2, 2)),
            dma((2, 2)),
            dma((4,)),
            dma((4,)),
        ],
        compiler_params=pltpu.CompilerParams(
            collective_id=0, has_side_effects=True, vmem_limit_bytes=60 * 1024 * 1024
        ),
        name="window",
    )(picks, cycle, stored, key_store, weight_local)
    wide_block = pl.BlockSpec((rows, features // 4), lambda n: (0, n))
    passed, owned = pl.pallas_call(
        finish,
        grid=(4,),
        out_shape=(
            jax.ShapeDtypeStruct(passed.shape, passed.dtype),
            jax.ShapeDtypeStruct((4 * piece_rows, width), jnp.float32),
        ),
        in_specs=[wide_block, pl.BlockSpec((1, tall, width), lambda n: (n, 0, 0))],
        out_specs=(wide_block, pl.BlockSpec((piece_rows, width), lambda n: (n, 0))),
        compiler_params=pltpu.CompilerParams(vmem_limit_bytes=60 * 1024 * 1024),
        name="finish",
    )(passed, pieces)
    return passed[None, None], owned[None]


def solution(mesh):
    placed = (
        P("dp", "pipe", None, "ctx", None),
        P("dp", "pipe", None, "ctx", None),
        P("pipe", "ctx", None),
        P("pipe"),
        P(),
    )
    return jax.shard_map(
        body,
        mesh=mesh,
        in_specs=placed,
        out_specs=(P("dp", "pipe", "ctx", None), P("pipe", "ctx", None)),
        check_vma=False,
    )
```
